32 devices in a mesh: grp: 4 (over y, x), seq: 8 (over z, core).
Axes of the slice: x: 2, y: 2, z: 4, core: 2. Of those that a mesh axis runs over, the one named last changes fastest.
Arguments:
- acoustic_sequence: bfloat16 [8192, 1536], P('seq'), may hold values from -6 to 6
- entry_rescale_factors: float32 [1536], replicated, may hold values from 0.1 to 1.9
- unitwise_entry_coefficients: bfloat16 [1536, 2, 1536], P(None, None, 'grp'), may hold values from -0.15625 to 0.15625
- channelwise_filter_taps: float32 [31, 1536], P(None, 'grp'), as said below
- filtering_rescale_factors: float32 [1536], P('grp'), may hold values from 0.1 to 1.9
- unitwise_exit_coefficients: bfloat16 [1536, 1536], P('grp'), may hold values from -0.15625 to 0.15625
- accumulation_coefficients: float32 [8192], P('seq'), may hold values from 0.03 to 0.3
- spike_indicator: int32 [8192], P('seq'), may hold values from 0 to 1, as said below
- textside_token_vectors: bfloat16 [1024, 4096], P('seq'), may hold values from -2 to 2
- textside_rescale_factors: float32 [4096], replicated, may hold values from 0.25 to 2.5
- probe_projection_coefficients: bfloat16 [4096, 2048], P(None, 'grp'), may hold values from -0.09375 to 0.09375
- probe_rescale_factors: float32 [128], replicated, may hold values from 0.5 to 1.5
- address_projection_coefficients: bfloat16 [1536, 512], P('grp'), may hold values from -0.15625 to 0.15625
- content_projection_coefficients: bfloat16 [1536, 512], P('grp'), may hold values from -0.15625 to 0.15625
- address_rescale_factors: float32 [128], replicated, may hold values from 0.25 to 2.5
- mixing_exit_coefficients: bfloat16 [2048, 4096], P('grp', 'seq'), may hold values from -0.125 to 0.125
Outputs:
- frames_out: bfloat16 [8192, 1536], P('seq', 'grp')
- pooled_out: bfloat16 [2048, 1536], P('seq', 'grp')
- dec_out: bfloat16 [1024, 4096], P('seq', 'grp')
The draws below stay inside these ranges and needn't reach their ends.
Inputs may be any that keep to these rules, and one draw needn't show every extreme that they name: `spike_indicator`: 1 marks the last frame of a pooled row; the last frame fires; each block of 1024 frames holds 1 to 255 firings, 1024 in all. `channelwise_filter_taps`: depthwise taps.
All inputs are finite; a program needn't handle non-finite values.
Results may differ from the reference program's by a relative error of at most 0.014.
Values may be sent and summed in bfloat16 or wider, within the bound.
A program may use at most 128 MiB of HBM per device.

```python
import math
import jax
import jax.numpy as jnp
from jax import lax

DC = 1536
KW = 31
DM = 4096
HEADS = 16
KVH = 4
HD = 128
STEPS_IN_PARTITN = 1024
SEG_DEV = 128
CAPL = 256
FRAMES = 8192
NSEG = 1024
TXT = 1024
N_SEQ = 8


def draw_channelwise_filter_taps(key, part):
    channel = jnp.arange(DC, dtype=jnp.float32) / DC
    raw_taps = jax.random.normal(key, (KW, DC), jnp.float32)
    spread = 3.0 ** channel
    return raw_taps * spread[None, :] * KW ** (-0.5)


def draw_spike_indicator(key, part):
    shards = FRAMES // STEPS_IN_PARTITN
    key_pair, key_delta, key_score = jax.random.split(key, 3)
    pairing = jax.random.permutation(key_pair, shards)
    deltas = jax.random.randint(key_delta, (shards // 2,), 0, SEG_DEV, dtype=jnp.int32)
    deltas = deltas.at[0].set(SEG_DEV - 1)
    counts = jnp.zeros((shards,), jnp.int32)
    counts = counts.at[pairing[0::2]].set(SEG_DEV + deltas)
    counts = counts.at[pairing[1::2]].set(SEG_DEV - deltas)
    scores = jax.random.randint(key_score, (shards, STEPS_IN_PARTITN), 0, 65536, dtype=jnp.int32) * STEPS_IN_PARTITN
    scores = scores + jnp.arange(STEPS_IN_PARTITN, dtype=jnp.int32)[None, :]
    scores = scores.at[shards - 1, STEPS_IN_PARTITN - 1].set(-1)
    ordering = jnp.argsort(scores, axis=1)
    ranking = jnp.argsort(ordering, axis=1)
    return (ranking < counts[:, None]).astype(jnp.int32).reshape(FRAMES)


def shard_levels(rng, extent, cuts, low, top_value):
    gain = 1.0
    for dim, blocks in cuts:
        heights = jax.random.uniform(jax.random.fold_in(jax.random.fold_in(rng, 6), dim), (blocks,), jnp.float32, low / len(cuts), top_value / len(cuts))
        gain = gain * jnp.repeat(jnp.exp(heights), extent[dim] // blocks).reshape((-1,) + (1,) * (len(extent) - 1 - dim))
    return gain


def normal_values(rng, extent, scale, bound, cuts=(), kind=jnp.bfloat16):
    gain = shard_levels(rng, extent, cuts, -0.22, 0.18) if cuts else 1.0
    array = jax.random.normal(rng, extent, jnp.float32) * scale * gain
    return jnp.minimum(jnp.maximum(array, -bound), bound).astype(kind)


def setup_inputs(seed: int = 0) -> dict:
    key_of = jax.random.split(jax.random.key(seed), 17)
    acoustic_sequence = normal_values(key_of[0], (FRAMES, DC), 1.0, 6.0, ((0, 8),))
    entry_rescale_factors = jnp.clip(1.0 + 0.18 * jax.random.normal(key_of[1], (DC,), jnp.float32), 0.1, 1.9)
    unitwise_entry_coefficients = normal_values(key_of[2], (DC, 2, DC), DC ** -0.5, 0.15625, ((2, 4),))
    channelwise_filter_taps = draw_channelwise_filter_taps(jax.random.fold_in(key_of[16], 71), 0)
    filtering_rescale_factors = jnp.clip(1.0 + 0.18 * jax.random.normal(key_of[4], (DC,), jnp.float32), 0.1, 1.9)
    unitwise_exit_coefficients = normal_values(key_of[5], (DC, DC), DC ** -0.5, 0.15625, ((0, 4),))
    accumulation_coefficients = jnp.clip(jnp.exp(math.log(0.3) - 2.3025852 * jax.random.uniform(key_of[6], (FRAMES,), jnp.float32) ** shard_levels(key_of[6], (FRAMES,), ((0, 8),), -0.2, 0.2)), 0.03, 0.3)
    spike_indicator = draw_spike_indicator(jax.random.fold_in(key_of[16], 71), 0)
    textside_token_vectors = normal_values(key_of[8], (TXT, DM), 0.3, 2.0, ((0, 8),))
    textside_rescale_factors = jnp.clip(jnp.exp(jax.random.uniform(key_of[9], (DM,), jnp.float32, math.log(0.25), math.log(2.5))), 0.25, 2.5)
    probe_projection_coefficients = normal_values(key_of[10], (DM, HEADS * HD), DM ** -0.5, 0.09375, ((1, 4),))
    probe_rescale_factors = jnp.clip(jnp.exp(jax.random.uniform(key_of[11], (HD,), jnp.float32, math.log(0.5), math.log(1.5))), 0.5, 1.5)
    address_projection_coefficients = normal_values(key_of[12], (DC, KVH * HD), DC ** -0.5, 0.15625, ((0, 4),))
    content_projection_coefficients = normal_values(key_of[13], (DC, KVH * HD), DC ** -0.5, 0.15625, ((0, 4),))
    address_rescale_factors = jnp.clip(jnp.exp(jax.random.uniform(key_of[14], (HD,), jnp.float32, math.log(0.25), math.log(2.5))), 0.25, 2.5)
    mixing_exit_coefficients = normal_values(key_of[15], (HEADS * HD, DM), (HEADS * HD) ** -0.5, 0.125, ((0, 4), (1, 8)))
    return dict(acoustic_sequence=acoustic_sequence, entry_rescale_factors=entry_rescale_factors, unitwise_entry_coefficients=unitwise_entry_coefficients, channelwise_filter_taps=channelwise_filter_taps, filtering_rescale_factors=filtering_rescale_factors, unitwise_exit_coefficients=unitwise_exit_coefficients, accumulation_coefficients=accumulation_coefficients, spike_indicator=spike_indicator, textside_token_vectors=textside_token_vectors, textside_rescale_factors=textside_rescale_factors, probe_projection_coefficients=probe_projection_coefficients, probe_rescale_factors=probe_rescale_factors, address_projection_coefficients=address_projection_coefficients, content_projection_coefficients=content_projection_coefficients, address_rescale_factors=address_rescale_factors, mixing_exit_coefficients=mixing_exit_coefficients)


EPS_LAYER = 1e-05
EPS_ROOT = 1e-06
SCORE_SCALE = 0.25

def layer_norm(inputs, scales):
    center = lax.optimization_barrier(jnp.mean(inputs, axis=-1, keepdims=True))
    variance = lax.optimization_barrier(jnp.mean((inputs - center) * (inputs - center), axis=-1, keepdims=True))
    return (inputs - center) * lax.rsqrt(variance + EPS_LAYER) * scales

def rms_scale(inputs, scales):
    return inputs * lax.rsqrt(lax.optimization_barrier(jnp.mean(inputs * inputs, axis=-1, keepdims=True)) + EPS_ROOT) * scales

def reference(acoustic_sequence, entry_rescale_factors, unitwise_entry_coefficients, channelwise_filter_taps, filtering_rescale_factors, unitwise_exit_coefficients, accumulation_coefficients, spike_indicator, textside_token_vectors, textside_rescale_factors, probe_projection_coefficients, probe_rescale_factors, address_projection_coefficients, content_projection_coefficients, address_rescale_factors, mixing_exit_coefficients):
    frames_f = acoustic_sequence.astype(jnp.float32)
    normed = layer_norm(frames_f, entry_rescale_factors).astype(jnp.bfloat16)
    projected = jnp.dot(normed, unitwise_entry_coefficients.reshape(DC, 2 * DC), preferred_element_type=jnp.float32).reshape(FRAMES, 2, DC)
    gated = (projected[:, 0] * jax.nn.sigmoid(projected[:, 1])).astype(jnp.bfloat16)
    padded = jnp.pad(gated.astype(jnp.float32), ((KW // 2, KW // 2), (0, 0)))
    mixed_conv = jnp.zeros((FRAMES, DC), jnp.float32)
    for tap_index in range(KW):
        mixed_conv = mixed_conv + channelwise_filter_taps[tap_index] * padded[tap_index:tap_index + FRAMES]
    normal_part = layer_norm(mixed_conv, filtering_rescale_factors)
    activated = (normal_part * jax.nn.sigmoid(normal_part)).astype(jnp.bfloat16)
    hidden = frames_f + jnp.dot(activated, unitwise_exit_coefficients, preferred_element_type=jnp.float32)
    frames_out = hidden.astype(jnp.bfloat16)
    interval_finder = (jnp.cumsum(spike_indicator) - spike_indicator).astype(jnp.int32)
    pooled = jax.ops.segment_sum(accumulation_coefficients[:, None] * hidden, interval_finder, num_segments=NSEG).astype(jnp.bfloat16)
    tally_within_group = lax.optimization_barrier(jnp.sum(spike_indicator.reshape(N_SEQ, STEPS_IN_PARTITN), axis=1)).astype(jnp.int32)
    block_starts = (jnp.cumsum(tally_within_group) - tally_within_group).astype(jnp.int32)
    slot_ids = jnp.arange(CAPL, dtype=jnp.int32)
    row_ids = block_starts[:, None] + slot_ids[None, :]
    is_valid = slot_ids[None, :] < tally_within_group[:, None]
    picked = pooled[jnp.minimum(row_ids, NSEG - 1).astype(jnp.int32)]
    pooled_out = jnp.where(is_valid[:, :, None], picked, jnp.zeros_like(picked)).reshape(N_SEQ * CAPL, DC)
    key_proj = jnp.dot(pooled, address_projection_coefficients, preferred_element_type=jnp.float32).reshape(NSEG, KVH, HD)
    keys = rms_scale(key_proj, address_rescale_factors).astype(jnp.bfloat16)
    values = jnp.dot(pooled, content_projection_coefficients, preferred_element_type=jnp.float32).astype(jnp.bfloat16).reshape(NSEG, KVH, HD)
    dec_normed = rms_scale(textside_token_vectors.astype(jnp.float32), textside_rescale_factors).astype(jnp.bfloat16)
    query_proj = jnp.dot(dec_normed, probe_projection_coefficients, preferred_element_type=jnp.float32).reshape(TXT, HEADS, HD)
    queries = rms_scale(query_proj, probe_rescale_factors).astype(jnp.bfloat16)
    query_heads = jnp.transpose(queries, (1, 0, 2))
    key_heads = jnp.transpose(keys, (1, 0, 2))
    value_heads = jnp.transpose(values, (1, 0, 2))
    group_size = HEADS // KVH

    def one_head(head_index):
        query_h = query_heads[head_index]
        key_h = key_heads[head_index // group_size]
        value_h = value_heads[head_index // group_size]
        scores = jnp.dot(query_h, key_h.T, preferred_element_type=jnp.float32) * SCORE_SCALE
        weights = jnp.exp(scores)
        numerator = jnp.dot(weights.astype(jnp.bfloat16), value_h, preferred_element_type=jnp.float32)
        return (numerator / lax.optimization_barrier(jnp.sum(weights, axis=1, keepdims=True))).astype(jnp.bfloat16)
    attended = lax.map(one_head, jnp.arange(HEADS, dtype=jnp.int32))
    attended = jnp.transpose(attended, (1, 0, 2)).reshape(TXT, HEADS * HD)
    dec_out = (textside_token_vectors.astype(jnp.float32) + jnp.dot(attended, mixing_exit_coefficients, preferred_element_type=jnp.float32)).astype(jnp.bfloat16)
    return (frames_out, pooled_out, dec_out)
```

```python
import functools

import jax
import jax.numpy as jnp
from jax import lax
from jax.experimental import pallas as pl
from jax.experimental.pallas import tpu as pltpu
from jax.sharding import PartitionSpec as P

CAPL = 256
EPS_LAYER = 1e-05
EPS_ROOT = 1e-06
SCORE_SCALE = 0.25
RIM = 16
MESH = pl.DeviceIdType.MESH


def exchange_kernel(axis, n, routes, *refs):
    m = len(routes)
    xs, outs = refs[:m], refs[m : 2 * m]
    send, recv, own = refs[2 * m :]
    me = lax.axis_index(axis)
    barrier = pltpu.get_barrier_semaphore()
    for k in range(1, n):
        pl.semaphore_signal(
            barrier, inc=1, device_id={axis: lax.rem(me + k, n)}, device_id_type=MESH
        )
    pl.semaphore_wait(barrier, n - 1)
    copies = []
    for i, (take, put) in enumerate(routes):
        for k in range(1, n):
            peer = lax.rem(me + k, n)
            copy = pltpu.make_async_remote_copy(
                src_ref=take(xs[i], peer),
                dst_ref=put(outs[i], me),
                send_sem=send.at[i, k],
                recv_sem=recv.at[i, k],
                device_id={axis: peer},
                device_id_type=MESH,
            )
            copy.start()
            copies.append(copy)
        mine = pltpu.make_async_copy(take(xs[i], me), put(outs[i], me), own.at[i])
        mine.start()
        copies.append(mine)
    for copy in copies:
        copy.wait()


def exchange(arrays, shapes, routes, axis, collective_id, name):
    n = lax.axis_size(axis)
    m = len(arrays)
    vmem = pl.BlockSpec(memory_space=pltpu.VMEM)
    return pl.pallas_call(
        functools.partial(exchange_kernel, axis, n, routes),
        out_shape=[jax.ShapeDtypeStruct(s, a.dtype) for s, a in zip(shapes, arrays)],
        in_specs=[vmem] * m,
        out_specs=[vmem] * m,
        scratch_shapes=[
            pltpu.SemaphoreType.DMA((m, n)),
            pltpu.SemaphoreType.DMA((m, n)),
            pltpu.SemaphoreType.DMA((m,)),
        ],
        compiler_params=pltpu.CompilerParams(
            collective_id=collective_id, has_side_effects=True
        ),
        name=name,
    )(*arrays)


def rows_at(size, length=None):
    length = length or size
    return lambda ref, i: ref.at[pl.ds(pl.multiple_of(i * size, size), length), :]


def cols_at(size):
    return lambda ref, i: ref.at[:, pl.ds(pl.multiple_of(i * size, size), size)]


def whole(ref, i):
    return ref


def slab(ref, i):
    return ref.at[i]


def gather_pairs_kernel(axis, n, x_ref, o_ref, send, recv, mate_send, mate_recv, own):
    rows = x_ref.shape[0]
    half = n // 2
    me = lax.axis_index(axis)
    mate = me + 1 - 2 * lax.rem(me, 2)

    def place(i):
        return o_ref.at[pl.ds(pl.multiple_of(i * rows, rows), rows), :]

    barrier = pltpu.get_barrier_semaphore()
    for k in range(1, half):
        pl.semaphore_signal(
            barrier, inc=1, device_id={axis: lax.rem(me + 2 * k, n)}, device_id_type=MESH
        )
    pl.semaphore_signal(barrier, inc=1, device_id={axis: mate}, device_id_type=MESH)
    pl.semaphore_wait(barrier, half)

    def over(src, dst, s, r, device):
        return pltpu.make_async_remote_copy(
            src_ref=src, dst_ref=dst, send_sem=s, recv_sem=r,
            device_id={axis: device}, device_id_type=MESH,
        )

    copies, forwards = [], []
    for k in range(1, half):
        copy = over(x_ref, place(me), send.at[k], recv.at[k], lax.rem(me + 2 * k, n))
        copy.start()
        copies.append(copy)
    first = over(x_ref, place(me), mate_send.at[0], mate_recv.at[0], mate)
    first.start()
    forwards.append(first)
    mine = pltpu.make_async_copy(x_ref, place(me), own)
    mine.start()
    for k in range(1, half):
        copies[k - 1].wait_recv()
        origin = lax.rem(me + n - 2 * k, n)
        hand = over(place(origin), place(origin), mate_send.at[k], mate_recv.at[k], mate)
        hand.start()
        forwards.append(hand)
    for hand in forwards:
        hand.wait()
    for copy in copies:
        copy.wait_send()
    mine.wait()


def gather_pairs(x, axis, collective_id, name):
    n = lax.axis_size(axis)
    vmem = pl.BlockSpec(memory_space=pltpu.VMEM)
    half = n // 2
    dma = pltpu.SemaphoreType.DMA
    return pl.pallas_call(
        functools.partial(gather_pairs_kernel, axis, n),
        out_shape=jax.ShapeDtypeStruct((n * x.shape[0], x.shape[1]), x.dtype),
        in_specs=[vmem],
        out_specs=vmem,
        scratch_shapes=[dma((half,)), dma((half,)), dma((half,)), dma((half,)), dma(())],
        compiler_params=pltpu.CompilerParams(
            collective_id=collective_id, has_side_effects=True
        ),
        name=name,
    )(x)


def layer_norm(inputs, scales):
    center = jnp.mean(inputs, axis=-1, keepdims=True)
    variance = jnp.mean((inputs - center) * (inputs - center), axis=-1, keepdims=True)
    return (inputs - center) * lax.rsqrt(variance + EPS_LAYER) * scales


def rms_scale(inputs, scales):
    return inputs * lax.rsqrt(jnp.mean(inputs * inputs, axis=-1, keepdims=True) + EPS_ROOT) * scales


def local(
    acoustic_sequence,
    entry_rescale_factors,
    unitwise_entry_coefficients,
    channelwise_filter_taps,
    filtering_rescale_factors,
    unitwise_exit_coefficients,
    accumulation_coefficients,
    spike_indicator,
    textside_token_vectors,
    textside_rescale_factors,
    probe_projection_coefficients,
    probe_rescale_factors,
    address_projection_coefficients,
    content_projection_coefficients,
    address_rescale_factors,
    mixing_exit_coefficients,
):
    frame_count, feature_width = acoustic_sequence.shape
    columns = unitwise_entry_coefficients.shape[2]
    groups = lax.axis_size("grp")
    blocks = lax.axis_size("seq")
    grp_index = lax.axis_index("grp")
    head_dim = probe_rescale_factors.shape[0]
    query_count, text_width = textside_token_vectors.shape
    share = frame_count // groups
    tap_total = channelwise_filter_taps.shape[0]
    f32, bf16 = jnp.float32, jnp.bfloat16

    exit_all = lax.all_gather(unitwise_exit_coefficients, "grp", axis=0, tiled=True)
    mixing_all = lax.all_gather(mixing_exit_coefficients, "seq", axis=1, tiled=True)

    before = lax.ppermute(
        acoustic_sequence[frame_count - RIM :], "seq", [(i, i + 1) for i in range(blocks - 1)]
    )
    after = lax.ppermute(
        acoustic_sequence[:RIM], "seq", [(i + 1, i) for i in range(blocks - 1)]
    )
    entry = unitwise_entry_coefficients.reshape(feature_width, 2 * columns)

    def gate(frames):
        normed = layer_norm(frames.astype(f32), entry_rescale_factors).astype(bf16)
        projected = jnp.dot(normed, entry, preferred_element_type=f32)
        return (projected[:, :columns] * jax.nn.sigmoid(projected[:, columns:])).astype(bf16)

    rims = gate(jnp.concatenate([before, after], axis=0))
    widened = jnp.concatenate([rims[:RIM], gate(acoustic_sequence), rims[RIM:]], axis=0)
    packed_taps = jnp.concatenate(
        [channelwise_filter_taps, filtering_rescale_factors[None, :]], axis=0
    )
    strip = share + 2 * RIM
    strips, taps_all = exchange(
        [widened, packed_taps],
        [(strip, feature_width), (tap_total + 1, feature_width)],
        [(rows_at(share, strip), cols_at(columns)), (whole, cols_at(columns))],
        "grp",
        1,
        "to_frames",
    )

    strips_f = strips.astype(f32)
    shift = RIM - tap_total // 2
    mixed_conv = jnp.zeros((share, feature_width), f32)
    for tap_index in range(tap_total):
        mixed_conv = mixed_conv + taps_all[tap_index] * strips_f[
            tap_index + shift : tap_index + shift + share
        ]
    normal_part = layer_norm(mixed_conv, taps_all[tap_total])
    activated = (normal_part * jax.nn.sigmoid(normal_part)).astype(bf16)
    residual_part = lax.dynamic_slice_in_dim(acoustic_sequence, grp_index * share, share, 0)
    hidden = (
        residual_part.astype(f32) + jnp.dot(activated, exit_all, preferred_element_type=f32)
    ).astype(bf16)
    (frames_out,) = exchange(
        [hidden],
        [(frame_count, columns)],
        [(cols_at(columns), rows_at(share))],
        "grp",
        2,
        "to_channels",
    )

    prior = jnp.cumsum(spike_indicator) - spike_indicator
    fired = jnp.sum(spike_indicator)
    weighted = accumulation_coefficients[:, None] * frames_out.astype(f32)
    slot_ids = jnp.arange(CAPL, dtype=jnp.int32)
    selector = (slot_ids[:, None] == prior[None, :]).astype(f32)
    sums = jnp.dot(selector, weighted, precision=lax.Precision.HIGHEST)
    tail_sum = lax.dynamic_slice_in_dim(sums, fired, 1, 0)
    carried = lax.ppermute(tail_sum, "seq", [(i, i + 1) for i in range(blocks - 1)])
    live = slot_ids[:, None] < fired
    pooled_local = jnp.where(
        live, sums + jnp.where(slot_ids[:, None] == 0, carried, 0.0), 0.0
    ).astype(bf16)

    kv_heads = address_projection_coefficients.shape[1] // head_dim
    key_part = jnp.dot(
        pooled_local, address_projection_coefficients, preferred_element_type=f32
    ).astype(bf16)
    value_part = jnp.dot(
        pooled_local, content_projection_coefficients, preferred_element_type=f32
    ).astype(bf16)
    (kv_parts,) = exchange(
        [jnp.stack([key_part, value_part])],
        [(groups, 2, CAPL, head_dim)],
        [
            (
                lambda ref, i: ref.at[
                    :, :, pl.ds(pl.multiple_of(i * head_dim, head_dim), head_dim)
                ],
                slab,
            )
        ],
        "grp",
        3,
        "kv_heads",
    )
    kv_mine = jnp.sum(kv_parts.astype(f32), axis=0)
    key_block = rms_scale(kv_mine[0], address_rescale_factors).astype(bf16)
    value_block = kv_mine[1].astype(bf16)
    note = jnp.concatenate(
        [jnp.zeros((16, head_dim), bf16), jnp.full((16, head_dim), fired, bf16)], axis=1
    )
    packed = jnp.concatenate(
        [jnp.concatenate([key_block, value_block], axis=1), note], axis=0
    )
    everyone = gather_pairs(packed, "seq", 4, "kv_rows")
    rows = CAPL + 16
    counts = everyone.reshape(blocks, rows, 2 * head_dim)[:, CAPL, head_dim]
    live_all = (
        jnp.arange(rows, dtype=jnp.int32)[None, :] < counts.astype(jnp.int32)[:, None]
    ).reshape(blocks * rows)

    dec_normed = rms_scale(
        textside_token_vectors.astype(f32), textside_rescale_factors
    ).astype(bf16)
    query_proj = jnp.dot(
        dec_normed, probe_projection_coefficients, preferred_element_type=f32
    ).reshape(query_count, -1, head_dim)
    queries = rms_scale(query_proj, probe_rescale_factors).astype(bf16)
    heads = queries.shape[1]
    queries = queries.transpose(1, 0, 2).reshape(heads * query_count, head_dim)
    scores = (
        lax.dot_general(
            queries, everyone[:, :head_dim], (((1,), (1,)), ((), ())), preferred_element_type=f32
        )
        * SCORE_SCALE
    )
    weights = jnp.where(live_all[None, :], jnp.exp(scores), 0.0)
    numerator = jnp.dot(
        weights.astype(bf16), everyone[:, head_dim:], preferred_element_type=f32
    )
    denominator = jnp.sum(weights, axis=-1, keepdims=True)
    attended = (
        (numerator / denominator)
        .astype(bf16)
        .reshape(heads, query_count, head_dim)
        .transpose(1, 0, 2)
        .reshape(query_count, heads * head_dim)
    )
    partial_out = jnp.dot(attended, mixing_all, preferred_element_type=f32).astype(bf16)
    out_width = text_width // groups
    (parts,) = exchange(
        [partial_out],
        [(groups, query_count, out_width)],
        [(cols_at(out_width), slab)],
        "grp",
        5,
        "dec_sums",
    )
    residual_dec = lax.dynamic_slice_in_dim(
        textside_token_vectors, grp_index * out_width, out_width, 1
    ).astype(f32)
    dec_out = (residual_dec + jnp.sum(parts.astype(f32), axis=0)).astype(bf16)
    return (frames_out, pooled_local, dec_out)


def solution(mesh):
    in_specs = (
        P("seq", None),
        P(),
        P(None, None, "grp"),
        P(None, "grp"),
        P("grp"),
        P("grp", None),
        P("seq"),
        P("seq"),
        P("seq", None),
        P(),
        P(None, "grp"),
        P(),
        P("grp", None),
        P("grp", None),
        P(),
        P("grp", "seq"),
    )
    out_specs = (P("seq", "grp"), P("seq", "grp"), P("seq", "grp"))
    return jax.shard_map(local, mesh=mesh, in_specs=in_specs, out_specs=out_specs, check_vma=False)
```

```python
import functools

import jax
import jax.numpy as jnp
from jax import lax
from jax.experimental import pallas as pl
from jax.experimental.pallas import tpu as pltpu
from jax.sharding import PartitionSpec as P

CAPL = 256
EPS_LAYER = 1e-05
EPS_ROOT = 1e-06
SCORE_SCALE = 0.25
RIM = 16
MESH = pl.DeviceIdType.MESH


def exchange_kernel(axis, n, routes, swap, *refs):
    m = len(routes)
    e = m + (swap is not None)
    xs, outs = refs[:e], refs[e : 2 * e]
    send, recv, own = refs[2 * e :]
    me = lax.axis_index(axis)
    barrier = pltpu.get_barrier_semaphore()
    if swap is not None:
        core = lax.rem(lax.axis_index(swap), 2)
        mate = lax.axis_index(swap) + 1 - 2 * core
        pl.semaphore_signal(barrier, inc=1, device_id={swap: mate}, device_id_type=MESH)
    for k in range(1, n):
        pl.semaphore_signal(
            barrier, inc=1, device_id={axis: lax.rem(me + k, n)}, device_id_type=MESH
        )
    pl.semaphore_wait(barrier, n - 1 + (swap is not None))
    copies = []
    if swap is not None:
        copy = pltpu.make_async_remote_copy(
            src_ref=xs[m],
            dst_ref=outs[m].at[:, core],
            send_sem=send.at[m, 0],
            recv_sem=recv.at[m, 0],
            device_id={swap: mate},
            device_id_type=MESH,
        )
        copy.start()
        copies.append(copy)
        mine = pltpu.make_async_copy(xs[m], outs[m].at[:, core], own.at[m])
        mine.start()
        copies.append(mine)
    for i, (take, put) in enumerate(routes):
        for k in range(1, n):
            peer = lax.rem(me + k, n)
            copy = pltpu.make_async_remote_copy(
                src_ref=take(xs[i], peer),
                dst_ref=put(outs[i], me),
                send_sem=send.at[i, k],
                recv_sem=recv.at[i, k],
                device_id={axis: peer},
                device_id_type=MESH,
            )
            copy.start()
            copies.append(copy)
        mine = pltpu.make_async_copy(take(xs[i], me), put(outs[i], me), own.at[i])
        mine.start()
        copies.append(mine)
    for copy in copies:
        copy.wait()


def exchange(arrays, shapes, routes, axis, collective_id, name, swap=None):
    n = lax.axis_size(axis)
    m = len(arrays)
    vmem = pl.BlockSpec(memory_space=pltpu.VMEM)
    return pl.pallas_call(
        functools.partial(exchange_kernel, axis, n, routes, swap),
        out_shape=[jax.ShapeDtypeStruct(s, a.dtype) for s, a in zip(shapes, arrays)],
        in_specs=[vmem] * m,
        out_specs=[vmem] * m,
        scratch_shapes=[
            pltpu.SemaphoreType.DMA((m, n)),
            pltpu.SemaphoreType.DMA((m, n)),
            pltpu.SemaphoreType.DMA((m,)),
        ],
        compiler_params=pltpu.CompilerParams(
            collective_id=collective_id, has_side_effects=True
        ),
        name=name,
    )(*arrays)


def rows_at(size, length=None):
    length = length or size
    return lambda ref, i: ref.at[pl.ds(pl.multiple_of(i * size, size), length), :]


def cols_at(size):
    return lambda ref, i: ref.at[:, pl.ds(pl.multiple_of(i * size, size), size)]


def whole(ref, i):
    return ref


def slab(ref, i):
    return ref.at[i]


def gather_pairs_kernel(axis, n, x_ref, o_ref, send, recv, mate_send, mate_recv, own):
    rows = x_ref.shape[0]
    half = n // 2
    me = lax.axis_index(axis)
    mate = me + 1 - 2 * lax.rem(me, 2)

    def place(i):
        return o_ref.at[pl.ds(pl.multiple_of(i * rows, rows), rows), :]

    barrier = pltpu.get_barrier_semaphore()
    for k in range(1, half):
        pl.semaphore_signal(
            barrier, inc=1, device_id={axis: lax.rem(me + 2 * k, n)}, device_id_type=MESH
        )
    pl.semaphore_signal(barrier, inc=1, device_id={axis: mate}, device_id_type=MESH)
    pl.semaphore_wait(barrier, half)

    def over(src, dst, s, r, device):
        return pltpu.make_async_remote_copy(
            src_ref=src, dst_ref=dst, send_sem=s, recv_sem=r,
            device_id={axis: device}, device_id_type=MESH,
        )

    copies, forwards = [], []
    for k in range(1, half):
        copy = over(x_ref, place(me), send.at[k], recv.at[k], lax.rem(me + 2 * k, n))
        copy.start()
        copies.append(copy)
    first = over(x_ref, place(me), mate_send.at[0], mate_recv.at[0], mate)
    first.start()
    forwards.append(first)
    mine = pltpu.make_async_copy(x_ref, place(me), own)
    mine.start()
    for k in range(1, half):
        copies[k - 1].wait_recv()
        origin = lax.rem(me + n - 2 * k, n)
        hand = over(place(origin), place(origin), mate_send.at[k], mate_recv.at[k], mate)
        hand.start()
        forwards.append(hand)
    for hand in forwards:
        hand.wait()
    for copy in copies:
        copy.wait_send()
    mine.wait()


def gather_pairs(x, axis, collective_id, name):
    n = lax.axis_size(axis)
    vmem = pl.BlockSpec(memory_space=pltpu.VMEM)
    half = n // 2
    dma = pltpu.SemaphoreType.DMA
    return pl.pallas_call(
        functools.partial(gather_pairs_kernel, axis, n),
        out_shape=jax.ShapeDtypeStruct((n * x.shape[0], x.shape[1]), x.dtype),
        in_specs=[vmem],
        out_specs=vmem,
        scratch_shapes=[dma((half,)), dma((half,)), dma((half,)), dma((half,)), dma(())],
        compiler_params=pltpu.CompilerParams(
            collective_id=collective_id, has_side_effects=True
        ),
        name=name,
    )(x)


def layer_norm(inputs, scales):
    center = jnp.mean(inputs, axis=-1, keepdims=True)
    variance = jnp.mean((inputs - center) * (inputs - center), axis=-1, keepdims=True)
    return (inputs - center) * lax.rsqrt(variance + EPS_LAYER) * scales


def rms_scale(inputs, scales):
    return inputs * lax.rsqrt(jnp.mean(inputs * inputs, axis=-1, keepdims=True) + EPS_ROOT) * scales


def local(
    acoustic_sequence,
    entry_rescale_factors,
    unitwise_entry_coefficients,
    channelwise_filter_taps,
    filtering_rescale_factors,
    unitwise_exit_coefficients,
    accumulation_coefficients,
    spike_indicator,
    textside_token_vectors,
    textside_rescale_factors,
    probe_projection_coefficients,
    probe_rescale_factors,
    address_projection_coefficients,
    content_projection_coefficients,
    address_rescale_factors,
    mixing_exit_coefficients,
):
    frame_count, feature_width = acoustic_sequence.shape
    columns = unitwise_entry_coefficients.shape[2]
    groups = lax.axis_size("grp")
    blocks = lax.axis_size("seq")
    grp_index = lax.axis_index("grp")
    head_dim = probe_rescale_factors.shape[0]
    query_count, text_width = textside_token_vectors.shape
    share = frame_count // groups
    tap_total = channelwise_filter_taps.shape[0]
    f32, bf16 = jnp.float32, jnp.bfloat16

    half_rows = unitwise_exit_coefficients.shape[0] // 2
    exit_half = lax.all_gather(
        lax.dynamic_slice_in_dim(
            unitwise_exit_coefficients,
            lax.rem(lax.axis_index("seq"), 2) * half_rows,
            half_rows,
            0,
        ),
        "grp",
        axis=0,
    )
    mixing_all = lax.all_gather(mixing_exit_coefficients, "seq", axis=1, tiled=True)

    before = lax.ppermute(
        acoustic_sequence[frame_count - RIM :], "seq", [(i, i + 1) for i in range(blocks - 1)]
    )
    after = lax.ppermute(
        acoustic_sequence[:RIM], "seq", [(i + 1, i) for i in range(blocks - 1)]
    )
    entry = unitwise_entry_coefficients.reshape(feature_width, 2 * columns)

    def gate(frames):
        normed = layer_norm(frames.astype(f32), entry_rescale_factors).astype(bf16)
        projected = jnp.dot(normed, entry, preferred_element_type=f32)
        return (projected[:, :columns] * jax.nn.sigmoid(projected[:, columns:])).astype(bf16)

    rims = gate(jnp.concatenate([before, after], axis=0))
    widened = jnp.concatenate([rims[:RIM], gate(acoustic_sequence), rims[RIM:]], axis=0)
    packed_taps = jnp.concatenate(
        [channelwise_filter_taps, filtering_rescale_factors[None, :]], axis=0
    )
    strip = share + 2 * RIM
    strips, taps_all, exit_all = exchange(
        [widened, packed_taps, exit_half],
        [
            (strip, feature_width),
            (tap_total + 1, feature_width),
            (groups, 2, half_rows, feature_width),
        ],
        [(rows_at(share, strip), cols_at(columns)), (whole, cols_at(columns))],
        "grp",
        1,
        "to_frames",
        swap="seq",
    )
    exit_all = exit_all.reshape(feature_width, feature_width)

    strips_f = strips.astype(f32)
    shift = RIM - tap_total // 2
    mixed_conv = jnp.zeros((share, feature_width), f32)
    for tap_index in range(tap_total):
        mixed_conv = mixed_conv + taps_all[tap_index] * strips_f[
            tap_index + shift : tap_index + shift + share
        ]
    normal_part = layer_norm(mixed_conv, taps_all[tap_total])
    activated = (normal_part * jax.nn.sigmoid(normal_part)).astype(bf16)
    residual_part = lax.dynamic_slice_in_dim(acoustic_sequence, grp_index * share, share, 0)
    hidden = (
        residual_part.astype(f32) + jnp.dot(activated, exit_all, preferred_element_type=f32)
    ).astype(bf16)
    (frames_out,) = exchange(
        [hidden],
        [(frame_count, columns)],
        [(cols_at(columns), rows_at(share))],
        "grp",
        2,
        "to_channels",
    )

    prior = jnp.cumsum(spike_indicator) - spike_indicator
    fired = jnp.sum(spike_indicator)
    weighted = accumulation_coefficients[:, None] * frames_out.astype(f32)
    slot_ids = jnp.arange(CAPL, dtype=jnp.int32)
    selector = (slot_ids[:, None] == prior[None, :]).astype(f32)
    sums = jnp.dot(selector, weighted, precision=lax.Precision.HIGHEST)
    tail_sum = lax.dynamic_slice_in_dim(sums, fired, 1, 0)
    carried = lax.ppermute(tail_sum, "seq", [(i, i + 1) for i in range(blocks - 1)])
    live = slot_ids[:, None] < fired
    pooled_local = jnp.where(
        live, sums + jnp.where(slot_ids[:, None] == 0, carried, 0.0), 0.0
    ).astype(bf16)

    kv_heads = address_projection_coefficients.shape[1] // head_dim
    key_part = jnp.dot(
        pooled_local, address_projection_coefficients, preferred_element_type=f32
    ).astype(bf16)
    value_part = jnp.dot(
        pooled_local, content_projection_coefficients, preferred_element_type=f32
    ).astype(bf16)
    (kv_parts,) = exchange(
        [jnp.stack([key_part, value_part])],
        [(groups, 2, CAPL, head_dim)],
        [
            (
                lambda ref, i: ref.at[
                    :, :, pl.ds(pl.multiple_of(i * head_dim, head_dim), head_dim)
                ],
                slab,
            )
        ],
        "grp",
        3,
        "kv_heads",
    )
    kv_mine = jnp.sum(kv_parts.astype(f32), axis=0)
    key_block = rms_scale(kv_mine[0], address_rescale_factors).astype(bf16)
    value_block = kv_mine[1].astype(bf16)
    note = jnp.concatenate(
        [jnp.zeros((16, head_dim), bf16), jnp.full((16, head_dim), fired, bf16)], axis=1
    )
    packed = jnp.concatenate(
        [jnp.concatenate([key_block, value_block], axis=1), note], axis=0
    )
    everyone = gather_pairs(packed, "seq", 4, "kv_rows")
    rows = CAPL + 16
    counts = everyone.reshape(blocks, rows, 2 * head_dim)[:, CAPL, head_dim]
    live_all = (
        jnp.arange(rows, dtype=jnp.int32)[None, :] < counts.astype(jnp.int32)[:, None]
    ).reshape(blocks * rows)

    dec_normed = rms_scale(
        textside_token_vectors.astype(f32), textside_rescale_factors
    ).astype(bf16)
    query_proj = jnp.dot(
        dec_normed, probe_projection_coefficients, preferred_element_type=f32
    ).reshape(query_count, -1, head_dim)
    queries = rms_scale(query_proj, probe_rescale_factors).astype(bf16)
    heads = queries.shape[1]
    queries = queries.transpose(1, 0, 2).reshape(heads * query_count, head_dim)
    scores = (
        lax.dot_general(
            queries, everyone[:, :head_dim], (((1,), (1,)), ((), ())), preferred_element_type=f32
        )
        * SCORE_SCALE
    )
    weights = jnp.where(live_all[None, :], jnp.exp(scores), 0.0)
    numerator = jnp.dot(
        weights.astype(bf16), everyone[:, head_dim:], preferred_element_type=f32
    )
    denominator = jnp.sum(weights, axis=-1, keepdims=True)
    attended = (
        (numerator / denominator)
        .astype(bf16)
        .reshape(heads, query_count, head_dim)
        .transpose(1, 0, 2)
        .reshape(query_count, heads * head_dim)
    )
    partial_out = jnp.dot(attended, mixing_all, preferred_element_type=f32).astype(bf16)
    out_width = text_width // groups
    (parts,) = exchange(
        [partial_out],
        [(groups, query_count, out_width)],
        [(cols_at(out_width), slab)],
        "grp",
        5,
        "dec_sums",
    )
    residual_dec = lax.dynamic_slice_in_dim(
        textside_token_vectors, grp_index * out_width, out_width, 1
    ).astype(f32)
    dec_out = (residual_dec + jnp.sum(parts.astype(f32), axis=0)).astype(bf16)
    return (frames_out, pooled_local, dec_out)


def solution(mesh):
    in_specs = (
        P("seq", None),
        P(),
        P(None, None, "grp"),
        P(None, "grp"),
        P("grp"),
        P("grp", None),
        P("seq"),
        P("seq"),
        P("seq", None),
        P(),
        P(None, "grp"),
        P(),
        P("grp", None),
        P("grp", None),
        P(),
        P("grp", "seq"),
    )
    out_specs = (P("seq", "grp"), P("seq", "grp"), P("seq", "grp"))
    return jax.shard_map(local, mesh=mesh, in_specs=in_specs, out_specs=out_specs, check_vma=False)
```

```python
import functools

import jax
import jax.numpy as jnp
from jax import lax
from jax.experimental import pallas as pl
from jax.experimental.pallas import tpu as pltpu
from jax.sharding import PartitionSpec as P

CAPL = 256
EPS_LAYER = 1e-05
EPS_ROOT = 1e-06
SCORE_SCALE = 0.25
RIM = 16
MESH = pl.DeviceIdType.MESH


def exchange_kernel(axis, n, routes, extra, *refs):
    m = len(routes)
    e_in, e_out = (extra[0], extra[1]) if extra else (0, 0)
    xs, outs = refs[:m], refs[m + e_in : 2 * m + e_in]
    send, recv, own = refs[2 * m + e_in + e_out :]
    me = lax.axis_index(axis)
    barrier = pltpu.get_barrier_semaphore()
    for k in range(1, n):
        pl.semaphore_signal(
            barrier, inc=1, device_id={axis: lax.rem(me + k, n)}, device_id_type=MESH
        )
    pl.semaphore_wait(barrier, n - 1)
    copies = []
    for i, (take, put) in enumerate(routes):
        for k in range(1, n):
            peer = lax.rem(me + k, n)
            copy = pltpu.make_async_remote_copy(
                src_ref=take(xs[i], peer),
                dst_ref=put(outs[i], me),
                send_sem=send.at[i, k],
                recv_sem=recv.at[i, k],
                device_id={axis: peer},
                device_id_type=MESH,
            )
            copy.start()
            copies.append(copy)
        mine = pltpu.make_async_copy(take(xs[i], me), put(outs[i], me), own.at[i])
        mine.start()
        copies.append(mine)
    if extra:
        extra[2](*refs[m : m + e_in], *refs[2 * m + e_in : 2 * m + e_in + e_out])
    for copy in copies:
        copy.wait()


def query_body(text_ref, scale_ref, probe_ref, gain_ref, out_ref):
    rows, width = text_ref.shape
    head_dim = gain_ref.shape[1]
    step = 512
    squares = jnp.zeros((rows, 1), jnp.float32)
    for c in range(0, width, step):
        x = text_ref[:, c : c + step].astype(jnp.float32)
        squares = squares + jnp.sum(x * x, axis=-1, keepdims=True)
    factor = lax.rsqrt(squares / width + EPS_ROOT)
    total = jnp.zeros((rows, probe_ref.shape[1]), jnp.float32)
    for c in range(0, width, step):
        x = text_ref[:, c : c + step].astype(jnp.float32)
        x = (x * factor * scale_ref[:, c : c + step]).astype(jnp.bfloat16)
        total = total + jnp.dot(x, probe_ref[c : c + step, :], preferred_element_type=jnp.float32)
    for h in range(total.shape[1] // head_dim):
        part = total[:, h * head_dim : (h + 1) * head_dim]
        part = part * lax.rsqrt(jnp.mean(part * part, axis=-1, keepdims=True) + EPS_ROOT)
        out_ref[h * rows : (h + 1) * rows, :] = (part * gain_ref[...]).astype(jnp.bfloat16)


def swap_kernel(axis, x_ref, o_ref, send, recv, own):
    core = lax.rem(lax.axis_index(axis), 2)
    mate = lax.axis_index(axis) + 1 - 2 * core
    barrier = pltpu.get_barrier_semaphore()
    pl.semaphore_signal(barrier, inc=1, device_id={axis: mate}, device_id_type=MESH)
    pl.semaphore_wait(barrier, 1)
    copy = pltpu.make_async_remote_copy(
        src_ref=x_ref, dst_ref=o_ref.at[:, core], send_sem=send, recv_sem=recv,
        device_id={axis: mate}, device_id_type=MESH,
    )
    copy.start()
    mine = pltpu.make_async_copy(x_ref, o_ref.at[:, core], own)
    mine.start()
    copy.wait()
    mine.wait()


def swap_halves(x, axis, collective_id, name):
    vmem = pl.BlockSpec(memory_space=pltpu.VMEM)
    dma = pltpu.SemaphoreType.DMA
    return pl.pallas_call(
        functools.partial(swap_kernel, axis),
        out_shape=jax.ShapeDtypeStruct((x.shape[0], 2) + x.shape[1:], x.dtype),
        in_specs=[vmem],
        out_specs=vmem,
        scratch_shapes=[dma(()), dma(()), dma(())],
        compiler_params=pltpu.CompilerParams(
            collective_id=collective_id, has_side_effects=True
        ),
        name=name,
    )(x)


def exchange(arrays, shapes, routes, axis, collective_id, name, operands=(), results=(), body=None):
    n = lax.axis_size(axis)
    m = len(arrays)
    vmem = pl.BlockSpec(memory_space=pltpu.VMEM)
    extra = (len(operands), len(results), body) if body else None
    return pl.pallas_call(
        functools.partial(exchange_kernel, axis, n, routes, extra),
        out_shape=[jax.ShapeDtypeStruct(s, a.dtype) for s, a in zip(shapes, arrays)]
        + list(results),
        in_specs=[vmem] * (m + len(operands)),
        out_specs=[vmem] * (m + len(results)),
        scratch_shapes=[
            pltpu.SemaphoreType.DMA((m, n)),
            pltpu.SemaphoreType.DMA((m, n)),
            pltpu.SemaphoreType.DMA((m,)),
        ],
        compiler_params=pltpu.CompilerParams(
            collective_id=collective_id, has_side_effects=True
        ),
        name=name,
    )(*arrays, *operands)


def rows_at(size, length=None):
    length = length or size
    return lambda ref, i: ref.at[pl.ds(pl.multiple_of(i * size, size), length), :]


def cols_at(size):
    return lambda ref, i: ref.at[:, pl.ds(pl.multiple_of(i * size, size), size)]


def whole(ref, i):
    return ref


def slab(ref, i):
    return ref.at[i]


def gather_pairs_kernel(axis, n, x_ref, o_ref, send, recv, mate_send, mate_recv, own):
    rows = x_ref.shape[0]
    chips = n // 2
    me = lax.axis_index(axis)
    chip = me // 2
    mate = me + 1 - 2 * lax.rem(me, 2)

    def place(i):
        return o_ref.at[pl.ds(pl.multiple_of(i * rows, rows), rows), :]

    def over(src, dst, s, r, device):
        return pltpu.make_async_remote_copy(
            src_ref=src, dst_ref=dst, send_sem=s, recv_sem=r,
            device_id={axis: device}, device_id_type=MESH,
        )

    up, down = lax.rem(me + 2, n), lax.rem(me + n - 2, n)
    has_up, has_down = chip < chips - 1, chip > 0
    barrier = pltpu.get_barrier_semaphore()
    pl.semaphore_signal(barrier, inc=1, device_id={axis: mate}, device_id_type=MESH)

    @pl.when(has_up)
    def _():
        pl.semaphore_signal(barrier, inc=1, device_id={axis: up}, device_id_type=MESH)

    @pl.when(has_down)
    def _():
        pl.semaphore_signal(barrier, inc=1, device_id={axis: down}, device_id_type=MESH)

    pl.semaphore_wait(barrier, 1 + has_up.astype(jnp.int32) + has_down.astype(jnp.int32))

    def hop(side, step, src):
        origin = me - 2 * step if side == 0 else me + 2 * step
        origin = lax.rem(origin + n, n)
        target = up if side == 0 else down
        source = src if src is not None else place(origin)
        return over(source, place(origin), send.at[side, step], recv.at[side, step], target)

    def sends(side, step):
        if side == 0:
            return jnp.logical_and(has_up, chip >= step)
        return jnp.logical_and(has_down, chip + step < chips)

    def arrives(side, step):
        return chip >= step + 1 if side == 0 else chip + step + 1 < chips

    def hand_on(side, step):
        origin = me - 2 * (step + 1) if side == 0 else me + 2 * (step + 1)
        spot = place(lax.rem(origin + n, n))
        return over(spot, spot, mate_send.at[side, step], mate_recv.at[side, step], mate)

    for side in range(2):

        @pl.when(sends(side, 0))
        def _(side=side):
            hop(side, 0, x_ref).start()

    first = over(x_ref, place(me), own.at[0], own.at[1], mate)
    first.start()
    mine = pltpu.make_async_copy(x_ref, place(me), own.at[2])
    mine.start()
    for step in range(chips - 1):
        for side in range(2):

            @pl.when(arrives(side, step))
            def _(side=side, step=step):
                hop(side, step, x_ref).wait_recv()

            if step + 1 < chips - 1:

                @pl.when(sends(side, step + 1))
                def _(side=side, step=step):
                    hop(side, step + 1, None).start()

            @pl.when(arrives(side, step))
            def _(side=side, step=step):
                hand_on(side, step).start()

    first.wait()
    mine.wait()
    for step in range(chips - 1):
        for side in range(2):

            @pl.when(arrives(side, step))
            def _(side=side, step=step):
                hand_on(side, step).wait()

            @pl.when(sends(side, step))
            def _(side=side, step=step):
                hop(side, step, x_ref).wait_send()


def gather_pairs(x, axis, collective_id, name):
    n = lax.axis_size(axis)
    vmem = pl.BlockSpec(memory_space=pltpu.VMEM)
    steps = n // 2 - 1
    dma = pltpu.SemaphoreType.DMA
    return pl.pallas_call(
        functools.partial(gather_pairs_kernel, axis, n),
        out_shape=jax.ShapeDtypeStruct((n * x.shape[0], x.shape[1]), x.dtype),
        in_specs=[vmem],
        out_specs=vmem,
        scratch_shapes=[dma((2, steps)), dma((2, steps)), dma((2, steps)), dma((2, steps)), dma((3,))],
        compiler_params=pltpu.CompilerParams(
            collective_id=collective_id, has_side_effects=True
        ),
        name=name,
    )(x)


def layer_norm(inputs, scales):
    center = jnp.mean(inputs, axis=-1, keepdims=True)
    variance = jnp.mean((inputs - center) * (inputs - center), axis=-1, keepdims=True)
    return (inputs - center) * lax.rsqrt(variance + EPS_LAYER) * scales


def rms_scale(inputs, scales):
    return inputs * lax.rsqrt(jnp.mean(inputs * inputs, axis=-1, keepdims=True) + EPS_ROOT) * scales


def local(
    acoustic_sequence,
    entry_rescale_factors,
    unitwise_entry_coefficients,
    channelwise_filter_taps,
    filtering_rescale_factors,
    unitwise_exit_coefficients,
    accumulation_coefficients,
    spike_indicator,
    textside_token_vectors,
    textside_rescale_factors,
    probe_projection_coefficients,
    probe_rescale_factors,
    address_projection_coefficients,
    content_projection_coefficients,
    address_rescale_factors,
    mixing_exit_coefficients,
):
    frame_count, feature_width = acoustic_sequence.shape
    columns = unitwise_entry_coefficients.shape[2]
    groups = lax.axis_size("grp")
    blocks = lax.axis_size("seq")
    grp_index = lax.axis_index("grp")
    head_dim = probe_rescale_factors.shape[0]
    query_count, text_width = textside_token_vectors.shape
    share = frame_count // groups
    tap_total = channelwise_filter_taps.shape[0]
    f32, bf16 = jnp.float32, jnp.bfloat16

    half_rows = unitwise_exit_coefficients.shape[0] // 2
    exit_half = lax.all_gather(
        lax.dynamic_slice_in_dim(
            unitwise_exit_coefficients,
            lax.rem(lax.axis_index("seq"), 2) * half_rows,
            half_rows,
            0,
        ),
        "grp",
        axis=0,
    )
    mixing_all = lax.all_gather(mixing_exit_coefficients, "seq", axis=1, tiled=True)

    before = lax.ppermute(
        acoustic_sequence[frame_count - RIM :], "seq", [(i, i + 1) for i in range(blocks - 1)]
    )
    after = lax.ppermute(
        acoustic_sequence[:RIM], "seq", [(i + 1, i) for i in range(blocks - 1)]
    )
    entry = unitwise_entry_coefficients.reshape(feature_width, 2 * columns)

    def gate(frames):
        normed = layer_norm(frames.astype(f32), entry_rescale_factors).astype(bf16)
        projected = jnp.dot(normed, entry, preferred_element_type=f32)
        return (projected[:, :columns] * jax.nn.sigmoid(projected[:, columns:])).astype(bf16)

    rims = gate(jnp.concatenate([before, after], axis=0))
    widened = jnp.concatenate([rims[:RIM], gate(acoustic_sequence), rims[RIM:]], axis=0)
    packed_taps = jnp.concatenate(
        [channelwise_filter_taps, filtering_rescale_factors[None, :]], axis=0
    )
    strip = share + 2 * RIM
    strips, taps_all = exchange(
        [widened, packed_taps],
        [(strip, feature_width), (tap_total + 1, feature_width)],
        [(rows_at(share, strip), cols_at(columns)), (whole, cols_at(columns))],
        "grp",
        1,
        "to_frames",
    )

    strips_f = strips.astype(f32)
    shift = RIM - tap_total // 2
    mixed_conv = jnp.zeros((share, feature_width), f32)
    for tap_index in range(tap_total):
        mixed_conv = mixed_conv + taps_all[tap_index] * strips_f[
            tap_index + shift : tap_index + shift + share
        ]
    normal_part = layer_norm(mixed_conv, taps_all[tap_total])
    activated = (normal_part * jax.nn.sigmoid(normal_part)).astype(bf16)
    exit_half, activated = lax.optimization_barrier((exit_half, activated))
    exit_all = swap_halves(exit_half, "seq", 6, "swap_halves").reshape(
        feature_width, feature_width
    )
    residual_part = lax.dynamic_slice_in_dim(acoustic_sequence, grp_index * share, share, 0)
    hidden = (
        residual_part.astype(f32) + jnp.dot(activated, exit_all, preferred_element_type=f32)
    ).astype(bf16)
    heads = probe_projection_coefficients.shape[1] // head_dim
    frames_out, queries = exchange(
        [hidden],
        [(frame_count, columns)],
        [(cols_at(columns), rows_at(share))],
        "grp",
        2,
        "to_channels",
        operands=[
            textside_token_vectors,
            textside_rescale_factors[None, :],
            probe_projection_coefficients,
            probe_rescale_factors[None, :],
        ],
        results=[jax.ShapeDtypeStruct((heads * query_count, head_dim), bf16)],
        body=query_body,
    )

    prior = jnp.cumsum(spike_indicator) - spike_indicator
    fired = jnp.sum(spike_indicator)
    weighted = accumulation_coefficients[:, None] * frames_out.astype(f32)
    slot_ids = jnp.arange(CAPL, dtype=jnp.int32)
    selector = (slot_ids[:, None] == prior[None, :]).astype(f32)
    sums = jnp.dot(selector, weighted, precision=lax.Precision.HIGHEST)
    tail_sum = lax.dynamic_slice_in_dim(sums, fired, 1, 0)
    carried = lax.ppermute(tail_sum, "seq", [(i, i + 1) for i in range(blocks - 1)])
    live = slot_ids[:, None] < fired
    pooled_local = jnp.where(
        live, sums + jnp.where(slot_ids[:, None] == 0, carried, 0.0), 0.0
    ).astype(bf16)

    kv_heads = address_projection_coefficients.shape[1] // head_dim
    key_part = jnp.dot(
        pooled_local, address_projection_coefficients, preferred_element_type=f32
    ).astype(bf16)
    value_part = jnp.dot(
        pooled_local, content_projection_coefficients, preferred_element_type=f32
    ).astype(bf16)
    (kv_parts,) = exchange(
        [jnp.stack([key_part, value_part])],
        [(groups, 2, CAPL, head_dim)],
        [
            (
                lambda ref, i: ref.at[
                    :, :, pl.ds(pl.multiple_of(i * head_dim, head_dim), head_dim)
                ],
                slab,
            )
        ],
        "grp",
        3,
        "kv_heads",
    )
    kv_mine = jnp.sum(kv_parts.astype(f32), axis=0)
    key_block = rms_scale(kv_mine[0], address_rescale_factors).astype(bf16)
    value_block = kv_mine[1].astype(bf16)
    note = jnp.concatenate(
        [jnp.zeros((16, head_dim), bf16), jnp.full((16, head_dim), fired, bf16)], axis=1
    )
    packed = jnp.concatenate(
        [jnp.concatenate([key_block, value_block], axis=1), note], axis=0
    )
    everyone = gather_pairs(packed, "seq", 4, "kv_rows")
    rows = CAPL + 16
    counts = everyone.reshape(blocks, rows, 2 * head_dim)[:, CAPL, head_dim]
    live_all = (
        jnp.arange(rows, dtype=jnp.int32)[None, :] < counts.astype(jnp.int32)[:, None]
    ).reshape(blocks * rows)

    scores = (
        lax.dot_general(
            queries, everyone[:, :head_dim], (((1,), (1,)), ((), ())), preferred_element_type=f32
        )
        * SCORE_SCALE
    )
    weights = jnp.where(live_all[None, :], jnp.exp(scores), 0.0)
    numerator = jnp.dot(
        weights.astype(bf16), everyone[:, head_dim:], preferred_element_type=f32
    )
    denominator = jnp.sum(weights, axis=-1, keepdims=True)
    attended = (
        (numerator / denominator)
        .astype(bf16)
        .reshape(heads, query_count, head_dim)
        .transpose(1, 0, 2)
        .reshape(query_count, heads * head_dim)
    )
    partial_out = jnp.dot(attended, mixing_all, preferred_element_type=f32).astype(bf16)
    out_width = text_width // groups
    (parts,) = exchange(
        [partial_out],
        [(groups, query_count, out_width)],
        [(cols_at(out_width), slab)],
        "grp",
        5,
        "dec_sums",
    )
    residual_dec = lax.dynamic_slice_in_dim(
        textside_token_vectors, grp_index * out_width, out_width, 1
    ).astype(f32)
    dec_out = (residual_dec + jnp.sum(parts.astype(f32), axis=0)).astype(bf16)
    return (frames_out, pooled_local, dec_out)


def solution(mesh):
    in_specs = (
        P("seq", None),
        P(),
        P(None, None, "grp"),
        P(None, "grp"),
        P("grp"),
        P("grp", None),
        P("seq"),
        P("seq"),
        P("seq", None),
        P(),
        P(None, "grp"),
        P(),
        P("grp", None),
        P("grp", None),
        P(),
        P("grp", "seq"),
    )
    out_specs = (P("seq", "grp"), P("seq", "grp"), P("seq", "grp"))
    return jax.shard_map(local, mesh=mesh, in_specs=in_specs, out_specs=out_specs, check_vma=False)
```

```python
import functools

import jax
import jax.numpy as jnp
from jax import lax
from jax.experimental import pallas as pl
from jax.experimental.pallas import tpu as pltpu
from jax.sharding import PartitionSpec as P

CAPL = 256
EPS_LAYER = 1e-05
EPS_ROOT = 1e-06
SCORE_SCALE = 0.25
RIM = 16
MESH = pl.DeviceIdType.MESH


def exchange_kernel(axis, n, routes, swap, *refs):
    m = len(routes)
    e = m + (swap is not None)
    xs, outs = refs[:e], refs[e : 2 * e]
    send, recv, own = refs[2 * e :]
    me = lax.axis_index(axis)
    barrier = pltpu.get_barrier_semaphore()
    if swap is not None:
        core = lax.rem(lax.axis_index(swap), 2)
        mate = lax.axis_index(swap) + 1 - 2 * core
        pl.semaphore_signal(barrier, inc=1, device_id={swap: mate}, device_id_type=MESH)
    for k in range(1, n):
        pl.semaphore_signal(
            barrier, inc=1, device_id={axis: lax.rem(me + k, n)}, device_id_type=MESH
        )
    pl.semaphore_wait(barrier, n - 1 + (swap is not None))
    copies = []
    if swap is not None:
        copy = pltpu.make_async_remote_copy(
            src_ref=xs[m],
            dst_ref=outs[m].at[:, core],
            send_sem=send.at[m, 0],
            recv_sem=recv.at[m, 0],
            device_id={swap: mate},
            device_id_type=MESH,
        )
        copy.start()
        copies.append(copy)
        mine = pltpu.make_async_copy(xs[m], outs[m].at[:, core], own.at[m])
        mine.start()
        copies.append(mine)
    for i, (take, put) in enumerate(routes):
        for k in range(1, n):
            peer = lax.rem(me + k, n)
            copy = pltpu.make_async_remote_copy(
                src_ref=take(xs[i], peer),
                dst_ref=put(outs[i], me),
                send_sem=send.at[i, k],
                recv_sem=recv.at[i, k],
                device_id={axis: peer},
                device_id_type=MESH,
            )
            copy.start()
            copies.append(copy)
        mine = pltpu.make_async_copy(take(xs[i], me), put(outs[i], me), own.at[i])
        mine.start()
        copies.append(mine)
    for copy in copies:
        copy.wait()


def exchange(arrays, shapes, routes, axis, collective_id, name, swap=None):
    n = lax.axis_size(axis)
    m = len(arrays)
    vmem = pl.BlockSpec(memory_space=pltpu.VMEM)
    return pl.pallas_call(
        functools.partial(exchange_kernel, axis, n, routes, swap),
        out_shape=[jax.ShapeDtypeStruct(s, a.dtype) for s, a in zip(shapes, arrays)],
        in_specs=[vmem] * m,
        out_specs=[vmem] * m,
        scratch_shapes=[
            pltpu.SemaphoreType.DMA((m, n)),
            pltpu.SemaphoreType.DMA((m, n)),
            pltpu.SemaphoreType.DMA((m,)),
        ],
        compiler_params=pltpu.CompilerParams(
            collective_id=collective_id, has_side_effects=True
        ),
        name=name,
    )(*arrays)


def product_kernel(axis, n, a_ref, w_ref, r_ref, o_ref, out_buf, parts, send, recv):
    width = parts.shape[2]
    me = lax.axis_index(axis)
    barrier = pltpu.get_barrier_semaphore()
    for k in range(1, n):
        pl.semaphore_signal(
            barrier, inc=1, device_id={axis: lax.rem(me + k, n)}, device_id_type=MESH
        )

    def product(i):
        columns = pl.ds(pl.multiple_of(i * width, width), width)
        return jnp.dot(a_ref[...], w_ref[:, columns], preferred_element_type=jnp.float32)

    copies = []
    for k in range(1, n):
        peer = lax.rem(me + k, n)
        out_buf[k - 1] = product(peer).astype(out_buf.dtype)
        if k == 1:
            pl.semaphore_wait(barrier, n - 1)
        copy = pltpu.make_async_remote_copy(
            src_ref=out_buf.at[k - 1],
            dst_ref=parts.at[k - 1],
            send_sem=send.at[k - 1],
            recv_sem=recv.at[k - 1],
            device_id={axis: peer},
            device_id_type=MESH,
        )
        copy.start()
        copies.append(copy)
    total = r_ref[...].astype(jnp.float32) + product(me)
    for k in range(1, n):
        copies[k - 1].wait()
        total = total + parts[k - 1].astype(jnp.float32)
    o_ref[...] = total.astype(o_ref.dtype)


def product_sum(a, w, r, axis, collective_id, name):
    n = lax.axis_size(axis)
    vmem = pl.BlockSpec(memory_space=pltpu.VMEM)
    dma = pltpu.SemaphoreType.DMA
    shape = (n - 1,) + r.shape
    return pl.pallas_call(
        functools.partial(product_kernel, axis, n),
        out_shape=jax.ShapeDtypeStruct(r.shape, r.dtype),
        in_specs=[vmem] * 3,
        out_specs=vmem,
        scratch_shapes=[
            pltpu.VMEM(shape, jnp.bfloat16),
            pltpu.VMEM(shape, jnp.bfloat16),
            dma((n - 1,)),
            dma((n - 1,)),
        ],
        compiler_params=pltpu.CompilerParams(
            collective_id=collective_id, has_side_effects=True
        ),
        name=name,
    )(a, w, r)


def rows_at(size, length=None):
    length = length or size
    return lambda ref, i: ref.at[pl.ds(pl.multiple_of(i * size, size), length), :]


def cols_at(size):
    return lambda ref, i: ref.at[:, pl.ds(pl.multiple_of(i * size, size), size)]


def whole(ref, i):
    return ref


def slab(ref, i):
    return ref.at[i]


def gather_pairs_kernel(axis, n, x_ref, o_ref, send, recv, mate_send, mate_recv, own):
    rows = x_ref.shape[0]
    half = n // 2
    me = lax.axis_index(axis)
    mate = me + 1 - 2 * lax.rem(me, 2)

    def place(i):
        return o_ref.at[pl.ds(pl.multiple_of(i * rows, rows), rows), :]

    barrier = pltpu.get_barrier_semaphore()
    for k in range(1, half):
        pl.semaphore_signal(
            barrier, inc=1, device_id={axis: lax.rem(me + 2 * k, n)}, device_id_type=MESH
        )
    pl.semaphore_signal(barrier, inc=1, device_id={axis: mate}, device_id_type=MESH)
    pl.semaphore_wait(barrier, half)

    def over(src, dst, s, r, device):
        return pltpu.make_async_remote_copy(
            src_ref=src, dst_ref=dst, send_sem=s, recv_sem=r,
            device_id={axis: device}, device_id_type=MESH,
        )

    copies, forwards = [], []
    for k in range(1, half):
        copy = over(x_ref, place(me), send.at[k], recv.at[k], lax.rem(me + 2 * k, n))
        copy.start()
        copies.append(copy)
    first = over(x_ref, place(me), mate_send.at[0], mate_recv.at[0], mate)
    first.start()
    forwards.append(first)
    mine = pltpu.make_async_copy(x_ref, place(me), own)
    mine.start()
    for k in range(1, half):
        copies[k - 1].wait_recv()
        origin = lax.rem(me + n - 2 * k, n)
        hand = over(place(origin), place(origin), mate_send.at[k], mate_recv.at[k], mate)
        hand.start()
        forwards.append(hand)
    for hand in forwards:
        hand.wait()
    for copy in copies:
        copy.wait_send()
    mine.wait()


def gather_pairs(x, axis, collective_id, name):
    n = lax.axis_size(axis)
    vmem = pl.BlockSpec(memory_space=pltpu.VMEM)
    half = n // 2
    dma = pltpu.SemaphoreType.DMA
    return pl.pallas_call(
        functools.partial(gather_pairs_kernel, axis, n),
        out_shape=jax.ShapeDtypeStruct((n * x.shape[0], x.shape[1]), x.dtype),
        in_specs=[vmem],
        out_specs=vmem,
        scratch_shapes=[dma((half,)), dma((half,)), dma((half,)), dma((half,)), dma(())],
        compiler_params=pltpu.CompilerParams(
            collective_id=collective_id, has_side_effects=True
        ),
        name=name,
    )(x)


def layer_norm(inputs, scales):
    center = jnp.mean(inputs, axis=-1, keepdims=True)
    variance = jnp.mean((inputs - center) * (inputs - center), axis=-1, keepdims=True)
    return (inputs - center) * lax.rsqrt(variance + EPS_LAYER) * scales


def rms_scale(inputs, scales):
    return inputs * lax.rsqrt(jnp.mean(inputs * inputs, axis=-1, keepdims=True) + EPS_ROOT) * scales


def local(
    acoustic_sequence,
    entry_rescale_factors,
    unitwise_entry_coefficients,
    channelwise_filter_taps,
    filtering_rescale_factors,
    unitwise_exit_coefficients,
    accumulation_coefficients,
    spike_indicator,
    textside_token_vectors,
    textside_rescale_factors,
    probe_projection_coefficients,
    probe_rescale_factors,
    address_projection_coefficients,
    content_projection_coefficients,
    address_rescale_factors,
    mixing_exit_coefficients,
):
    frame_count, feature_width = acoustic_sequence.shape
    columns = unitwise_entry_coefficients.shape[2]
    groups = lax.axis_size("grp")
    blocks = lax.axis_size("seq")
    grp_index = lax.axis_index("grp")
    head_dim = probe_rescale_factors.shape[0]
    query_count, text_width = textside_token_vectors.shape
    share = frame_count // groups
    tap_total = channelwise_filter_taps.shape[0]
    f32, bf16 = jnp.float32, jnp.bfloat16

    half_rows = unitwise_exit_coefficients.shape[0] // 2
    exit_half = lax.all_gather(
        lax.dynamic_slice_in_dim(
            unitwise_exit_coefficients,
            lax.rem(lax.axis_index("seq"), 2) * half_rows,
            half_rows,
            0,
        ),
        "grp",
        axis=0,
    )
    mixing_all = lax.all_gather(mixing_exit_coefficients, "seq", axis=1, tiled=True)

    before = lax.ppermute(
        acoustic_sequence[frame_count - RIM :], "seq", [(i, i + 1) for i in range(blocks - 1)]
    )
    after = lax.ppermute(
        acoustic_sequence[:RIM], "seq", [(i + 1, i) for i in range(blocks - 1)]
    )
    entry = unitwise_entry_coefficients.reshape(feature_width, 2 * columns)

    def gate(frames):
        normed = layer_norm(frames.astype(f32), entry_rescale_factors).astype(bf16)
        projected = jnp.dot(normed, entry, preferred_element_type=f32)
        return (projected[:, :columns] * jax.nn.sigmoid(projected[:, columns:])).astype(bf16)

    rims = gate(jnp.concatenate([before, after], axis=0))
    widened = jnp.concatenate([rims[:RIM], gate(acoustic_sequence), rims[RIM:]], axis=0)
    packed_taps = jnp.concatenate(
        [channelwise_filter_taps, filtering_rescale_factors[None, :]], axis=0
    )
    strip = share + 2 * RIM
    strips, taps_all, exit_all = exchange(
        [widened, packed_taps, exit_half],
        [
            (strip, feature_width),
            (tap_total + 1, feature_width),
            (groups, 2, half_rows, feature_width),
        ],
        [(rows_at(share, strip), cols_at(columns)), (whole, cols_at(columns))],
        "grp",
        1,
        "to_frames",
        swap="seq",
    )
    exit_all = exit_all.reshape(feature_width, feature_width)

    strips_f = strips.astype(f32)
    shift = RIM - tap_total // 2
    mixed_conv = jnp.zeros((share, feature_width), f32)
    for tap_index in range(tap_total):
        mixed_conv = mixed_conv + taps_all[tap_index] * strips_f[
            tap_index + shift : tap_index + shift + share
        ]
    normal_part = layer_norm(mixed_conv, taps_all[tap_total])
    activated = (normal_part * jax.nn.sigmoid(normal_part)).astype(bf16)
    residual_part = lax.dynamic_slice_in_dim(acoustic_sequence, grp_index * share, share, 0)
    hidden = (
        residual_part.astype(f32) + jnp.dot(activated, exit_all, preferred_element_type=f32)
    ).astype(bf16)
    (frames_out,) = exchange(
        [hidden],
        [(frame_count, columns)],
        [(cols_at(columns), rows_at(share))],
        "grp",
        2,
        "to_channels",
    )

    prior = jnp.cumsum(spike_indicator) - spike_indicator
    fired = jnp.sum(spike_indicator)
    weighted = accumulation_coefficients[:, None] * frames_out.astype(f32)
    slot_ids = jnp.arange(CAPL, dtype=jnp.int32)
    selector = (slot_ids[:, None] == prior[None, :]).astype(f32)
    sums = jnp.dot(selector, weighted, precision=lax.Precision.HIGHEST)
    tail_sum = lax.dynamic_slice_in_dim(sums, fired, 1, 0)
    carried = lax.ppermute(tail_sum, "seq", [(i, i + 1) for i in range(blocks - 1)])
    live = slot_ids[:, None] < fired
    pooled_local = jnp.where(
        live, sums + jnp.where(slot_ids[:, None] == 0, carried, 0.0), 0.0
    ).astype(bf16)

    kv_heads = address_projection_coefficients.shape[1] // head_dim
    key_part = jnp.dot(
        pooled_local, address_projection_coefficients, preferred_element_type=f32
    ).astype(bf16)
    value_part = jnp.dot(
        pooled_local, content_projection_coefficients, preferred_element_type=f32
    ).astype(bf16)
    (kv_parts,) = exchange(
        [jnp.stack([key_part, value_part])],
        [(groups, 2, CAPL, head_dim)],
        [
            (
                lambda ref, i: ref.at[
                    :, :, pl.ds(pl.multiple_of(i * head_dim, head_dim), head_dim)
                ],
                slab,
            )
        ],
        "grp",
        3,
        "kv_heads",
    )
    kv_mine = jnp.sum(kv_parts.astype(f32), axis=0)
    key_block = rms_scale(kv_mine[0], address_rescale_factors).astype(bf16)
    value_block = kv_mine[1].astype(bf16)
    note = jnp.concatenate(
        [jnp.zeros((16, head_dim), bf16), jnp.full((16, head_dim), fired, bf16)], axis=1
    )
    packed = jnp.concatenate(
        [jnp.concatenate([key_block, value_block], axis=1), note], axis=0
    )
    everyone = gather_pairs(packed, "seq", 4, "kv_rows")
    rows = CAPL + 16
    counts = everyone.reshape(blocks, rows, 2 * head_dim)[:, CAPL, head_dim]
    live_all = (
        jnp.arange(rows, dtype=jnp.int32)[None, :] < counts.astype(jnp.int32)[:, None]
    ).reshape(blocks * rows)

    dec_normed = rms_scale(
        textside_token_vectors.astype(f32), textside_rescale_factors
    ).astype(bf16)
    query_proj = jnp.dot(
        dec_normed, probe_projection_coefficients, preferred_element_type=f32
    ).reshape(query_count, -1, head_dim)
    queries = rms_scale(query_proj, probe_rescale_factors).astype(bf16)
    heads = queries.shape[1]
    queries = queries.transpose(1, 0, 2).reshape(heads * query_count, head_dim)
    scores = (
        lax.dot_general(
            queries, everyone[:, :head_dim], (((1,), (1,)), ((), ())), preferred_element_type=f32
        )
        * SCORE_SCALE
    )
    weights = jnp.where(live_all[None, :], jnp.exp(scores), 0.0)
    numerator = jnp.dot(
        weights.astype(bf16), everyone[:, head_dim:], preferred_element_type=f32
    )
    denominator = jnp.sum(weights, axis=-1, keepdims=True)
    attended = (
        (numerator / denominator)
        .astype(bf16)
        .reshape(heads, query_count, head_dim)
        .transpose(1, 0, 2)
        .reshape(query_count, heads * head_dim)
    )
    out_width = text_width // groups
    residual_dec = lax.dynamic_slice_in_dim(
        textside_token_vectors, grp_index * out_width, out_width, 1
    )
    dec_out = product_sum(attended, mixing_all, residual_dec, "grp", 5, "dec_sums")
    return (frames_out, pooled_local, dec_out)


def solution(mesh):
    in_specs = (
        P("seq", None),
        P(),
        P(None, None, "grp"),
        P(None, "grp"),
        P("grp"),
        P("grp", None),
        P("seq"),
        P("seq"),
        P("seq", None),
        P(),
        P(None, "grp"),
        P(),
        P("grp", None),
        P("grp", None),
        P(),
        P("grp", "seq"),
    )
    out_specs = (P("seq", "grp"), P("seq", "grp"), P("seq", "grp"))
    return jax.shard_map(local, mesh=mesh, in_specs=in_specs, out_specs=out_specs, check_vma=False)
```
